128 devices in a mesh: grp: 8 (over z_hi, x), aux: 16 (over y, z_lo, core).
Axes of the slice: x: 4, y: 4, z: 4 (z_hi: 2, z_lo: 2; z = z_hi * 2 + z_lo), core: 2. Of those that a mesh axis runs over, the one named last changes fastest.
Arguments:
- integrals: float32 [1536, 256, 384], P('aux', 'grp'), may hold values from -0.8 to 0.8
- occ_energy: float32 [256], replicated, may hold values from -2 to -0.3
- vir_energy: float32 [384], replicated, may hold values from 0.2 to 3
- orbital_order: int32 [256], replicated, may hold values from 0 to 255, each once
- owners: int32 [1, 8], replicated, may hold values from 0 to 15, as said below
Outputs:
- density: float32 [1536, 256, 384], P('aux', 'grp')
The draws below stay inside these ranges and needn't reach their ends.
Inputs may be any that keep to these rules, and one draw needn't show every extreme that they name: `orbital_order`: a permutation of the table's entries. owners[s, g] names one of the 16 blocks of the group before g.
All inputs are finite; a program needn't handle non-finite values.
Results may differ from the reference program's by a relative error of at most 0.00011.
Values sent between devices are 32-bit elements; how exact they have to be, the bound alone decides.
A program may use at most 64 MiB of HBM per device.

```python
import jax
import jax.numpy as jnp
from jax import lax

NAUX = 1536
NOCC = 256
NVIR = 384
STEPS = 1
N_GRP = 8
N_AUX = 16


def draw_owners(key, part):
    total = STEPS * N_GRP
    first_key = jax.random.fold_in(key, 11)
    second_key = jax.random.fold_in(key, 12)
    third_key = jax.random.fold_in(key, 13)
    values = jax.random.randint(first_key, (total,), 0, N_AUX, dtype=jnp.int32)
    high_spot = jax.random.randint(second_key, (), 0, total, dtype=jnp.int32)
    offset = jax.random.randint(third_key, (), 1, total, dtype=jnp.int32)
    low_spot = (high_spot + offset) % total
    places = jnp.arange(total, dtype=jnp.int32)
    values = jnp.where(places == high_spot, N_AUX - 1, values)
    values = jnp.where(places == low_spot, 0, values)
    return values.reshape(STEPS, N_GRP).astype(jnp.int32)


def shard_levels(stream_key, extent, cuts, smallest, largest):
    def one(axis_at, shards_of):
        heights = jax.random.uniform(jax.random.fold_in(jax.random.fold_in(stream_key, 6), axis_at), (shards_of,), jnp.float32, smallest / len(cuts), largest / len(cuts))
        return jnp.repeat(jnp.exp(heights), extent[axis_at] // shards_of).reshape((-1,) + (1,) * (len(extent) - axis_at - 1))

    level = one(*cuts[0])
    for cut in cuts[1:]:
        level = level * one(*cut)
    return level


def noise(own_key, dims, scale, most, cuts=(), kind=jnp.bfloat16):
    array = jax.random.normal(own_key, dims, jnp.float32) * scale
    if len(cuts) > 0:
        array = shard_levels(own_key, dims, cuts, -0.22, 0.18) * array
    return jnp.clip(array, min=-most, max=most).astype(kind)


def setup_inputs(seed: int = 0) -> dict:
    arg_keys = jax.random.split(jax.random.key(seed), 6)
    integrals = noise(arg_keys[0], (NAUX, NOCC, NVIR), 0.1, 0.8, ((0, 16), (1, 8)), jnp.float32)
    occ_energy = jnp.clip(jax.random.uniform(arg_keys[1], (NOCC,), jnp.float32, -2.0, -0.3), -2.0, -0.3)
    vir_energy = jnp.clip(jax.random.uniform(arg_keys[2], (NVIR,), jnp.float32, 0.2, 3.0), 0.2, 3.0)
    orbital_order = jax.random.permutation(arg_keys[3], NOCC).astype(jnp.int32)
    owners = draw_owners(jax.random.fold_in(arg_keys[5], 71), 0)
    return dict(integrals=integrals, occ_energy=occ_energy, vir_energy=vir_energy, orbital_order=orbital_order, owners=owners)


level_shift = 0.5


def reference(integrals, occ_energy, vir_energy, orbital_order, owners):
    highest = lax.Precision.HIGHEST
    levels = jnp.take(occ_energy, orbital_order)
    group_occ = NOCC // N_GRP
    occ_block = NOCC // (N_GRP * N_AUX)
    results = []
    for group in range(N_GRP):
        source = (group - 1) % N_GRP
        mine = integrals[:, group * group_occ:(group + 1) * group_occ, :]
        theirs = integrals[:, source * group_occ:(source + 1) * group_occ, :]
        mine_levels = levels[group * group_occ:(group + 1) * group_occ]
        their_levels = levels[source * group_occ:(source + 1) * group_occ]
        density = jnp.zeros((NAUX, group_occ, NVIR), jnp.float32)
        for step in range(STEPS):
            start = (owners[step, group] * occ_block).astype(jnp.int32)
            j_block = lax.dynamic_slice_in_dim(theirs, start, occ_block, 1)
            j_levels = lax.dynamic_slice_in_dim(their_levels, start, occ_block, 0)
            pair_ints = jnp.einsum("pia,pjb->iajb", mine, j_block, precision=highest)
            swapped = jnp.transpose(pair_ints, (0, 3, 2, 1))
            gaps = (vir_energy[None, :, None, None] + vir_energy[None, None, None, :]
                    - mine_levels[:, None, None, None] - j_levels[None, None, :, None] + level_shift)
            amplitude = (2.0 * pair_ints - swapped) / gaps
            density = density + jnp.einsum("iajb,pjb->pia", amplitude, j_block, precision=highest)
        results.append(density)
    return jnp.concatenate(results, axis=1)
```

```python
import jax
import jax.numpy as jnp
from jax import lax
from jax.sharding import PartitionSpec as P

level_shift = 0.5


def body(integrals, occ_energy, vir_energy, orbital_order, owners):
    highest = lax.Precision.HIGHEST
    high = lax.Precision.HIGH
    n_groups = lax.axis_size("grp")
    n_aux = lax.axis_size("aux")
    grp_index = lax.axis_index("grp")
    aux_index = lax.axis_index("aux")
    group_occ = integrals.shape[1]
    n_vir = integrals.shape[2]
    n_occ = occ_energy.shape[0]
    occ_block = group_occ // n_aux
    owner_now = owners[0, grp_index]
    next_owner = owners[0, (grp_index + 1) % n_groups]
    cut = lax.dynamic_slice_in_dim(integrals, next_owner * occ_block, occ_block, 1)
    cut = lax.ppermute(cut, "grp", [(i, (i + 1) % n_groups) for i in range(n_groups)])
    j_block = lax.all_gather(cut, "aux", axis=0, tiled=True)
    owned = lax.all_to_all(integrals, "aux", split_axis=1, concat_axis=0, tiled=True)
    n_auxfun = owned.shape[0]
    mine_flat = owned.reshape(n_auxfun, occ_block * n_vir)
    onehot = (orbital_order[:, None] == jnp.arange(n_occ, dtype=jnp.int32)[None, :]).astype(
        jnp.float32
    )
    levels = jnp.dot(onehot, occ_energy, precision=highest, preferred_element_type=jnp.float32)
    mine_start = grp_index * group_occ + aux_index * occ_block
    mine_levels = lax.dynamic_slice_in_dim(levels, mine_start, occ_block, 0)
    source_group = (grp_index + n_groups - 1) % n_groups
    vir_pair = vir_energy[None, :, None, None] + vir_energy[None, None, None, :]
    j_flat = j_block.reshape(n_auxfun, occ_block * n_vir)
    j_levels = lax.dynamic_slice_in_dim(
        levels, source_group * group_occ + owner_now * occ_block, occ_block, 0
    )
    pair_flat = lax.dot_general(
        mine_flat, j_flat, (((0,), (0,)), ((), ())), precision=high,
        preferred_element_type=jnp.float32,
    )
    pair_ints = pair_flat.reshape(occ_block, n_vir, occ_block, n_vir)
    swapped = jnp.transpose(pair_ints, (0, 3, 2, 1))
    gaps = vir_pair - mine_levels[:, None, None, None] - j_levels[None, None, :, None] + level_shift
    amplitude = ((2.0 * pair_ints - swapped) / gaps).reshape(occ_block * n_vir, occ_block * n_vir)
    density = lax.dot_general(
        j_flat, amplitude, (((1,), (1,)), ((), ())), precision=high,
        preferred_element_type=jnp.float32,
    )
    density = density.reshape(n_auxfun, occ_block, n_vir)
    return lax.all_to_all(density, "aux", split_axis=0, concat_axis=1, tiled=True)


def solution(mesh):
    in_specs = (P("aux", "grp", None), P(), P(), P(), P())
    out_specs = P("aux", "grp", None)
    return jax.shard_map(body, mesh=mesh, in_specs=in_specs, out_specs=out_specs, check_vma=False)
```

```python
import jax
import jax.numpy as jnp
from jax import lax
from jax.experimental import pallas as pl
from jax.experimental.pallas import tpu as pltpu
from jax.sharding import PartitionSpec as P

level_shift = 0.5
MESH = pl.DeviceIdType.MESH

ROUTE = (
    (1, 0, 0), (3, 1, 0), (2, 1, 0), (0, 1, 0), (2, 0, 0),
    (1, 1, 0), (3, 0, 0), (0, 0, 1), (1, 0, 1), (3, 1, 1),
    (2, 1, 1), (0, 1, 1), (2, 0, 1), (1, 1, 1), (3, 0, 1),
)


def split(x):
    hi = x.astype(jnp.bfloat16)
    lo = (x - hi.astype(jnp.float32)).astype(jnp.bfloat16)
    return hi, lo


def kernel(sizes, occ, order, owners, vir, in_hbm, out, rows_in, staged, held, jblock, jcut, jhi, jlo,
           jthi, jtlo, xhi, xlo, acc, ahi, alo, vsum, dens, back, load_sem, jsend, jrecv, xsend, xrecv,
           osend, orecv):
    n_grp, n_aux, depth, n_occ, n_vir, occ_block = sizes
    chunk = 4 * depth
    grp = lax.axis_index("grp")
    me = lax.axis_index("aux")
    y, z, c = lax.div(me, 4), lax.rem(lax.div(me, 2), 2), lax.rem(me, 2)
    nxt = lax.rem(grp + 1, n_grp)
    prv = lax.rem(grp + n_grp - 1, n_grp)

    def dev(dy, dz, dc):
        return lax.rem(y + dy, 4) * 4 + lax.rem(z + dz, 2) * 2 + lax.rem(c + dc, 2)

    def rows(a):
        return pl.ds(pl.multiple_of(a * depth, 8), depth)

    lanes = range(n_vir // 128)
    loads = [pltpu.make_async_copy(in_hbm.at[:, n * 128:(n + 1) * 128], rows_in.at[n], load_sem.at[n]) for n in lanes]
    for load in loads:
        load.start()
    barrier = pltpu.get_barrier_semaphore()
    for n in range(1, 16):
        pl.semaphore_signal(barrier, inc=1, device_id=(grp, lax.rem(me + n, 16)), device_id_type=MESH)
    pl.semaphore_signal(barrier, inc=1, device_id=(nxt, me), device_id_type=MESH)
    pl.semaphore_signal(barrier, inc=1, device_id=(prv, me), device_id_type=MESH)

    wide = jnp.broadcast_to(vir[...], (n_vir, n_vir))
    vsum[...] = wide + wide.T
    for load in loads:
        load.wait()

    picked = owners[0, nxt] * occ_block
    for k in range(occ_block):
        for n in lanes:
            at = k * n_vir + n * 128
            jcut[:, at:at + 128] = rows_in[n, pl.ds(picked + k, depth, stride=n_occ), :]
    pl.semaphore_wait(barrier, 17)

    def jcopy(n, a, target, src=None):
        return pltpu.make_async_remote_copy(
            src_ref=jblock.at[rows(a), :] if src is None else src, dst_ref=jblock.at[rows(a), :],
            send_sem=jsend.at[n], recv_sem=jrecv.at[a], device_id=target, device_id_type=MESH)

    def xcopy(k, n, a, target):
        return pltpu.make_async_remote_copy(
            src_ref=staged.at[k, rows(target), :], dst_ref=held.at[k, rows(a), :],
            send_sem=xsend.at[k, n], recv_sem=xrecv.at[k, a], device_id=(grp, target), device_id_type=MESH)

    def ocopy(k, n, a, target):
        return pltpu.make_async_remote_copy(
            src_ref=dens.at[k, rows(target), :], dst_ref=back.at[k, rows(a), :],
            send_sem=osend.at[k, n], recv_sem=orecv.at[k, a], device_id=(grp, target), device_id_type=MESH)

    for d in range(n_aux):
        for k in range(occ_block):
            for n in lanes:
                staged[k, d * depth:(d + 1) * depth, n * 128:(n + 1) * 128] = rows_in[
                    n, pl.ds(d * occ_block + k, depth, stride=n_occ), :]
        if d == 0:
            jcopy(0, me, (nxt, me), jcut).start()
    for k in range(occ_block):
        held[k, rows(me), :] = staged[k, rows(me), :]

    xorder = [(k, n) for k in range(occ_block) for n in range(len(ROUTE))]
    xplace = [0]

    def xsend_some(count):
        for k, n in xorder[xplace[0]:xplace[0] + count]:
            xcopy(k, n, me, dev(*ROUTE[n])).start()
        xplace[0] += count

    steps = [0]
    up, down, over, twin = dev(1, 0, 0), dev(3, 0, 0), dev(0, 1, 0), dev(0, 0, 1)
    sent = []

    def jrelay(a, targets):
        jcopy(0, a, (grp, twin)).wait_recv()
        for t in tuple(targets) + (twin,):
            steps[0] += 1
            copy = jcopy(steps[0], a, (grp, t))
            copy.start()
            sent.append(copy)

    xsend_some(4)
    jrelay(me, (over, up, down))
    xsend_some(3)
    jrelay(over, (up, down))
    xsend_some(3)
    jrelay(down, (up,))
    jrelay(dev(1, 1, 0), (down,))
    xsend_some(5)
    jrelay(up, ())
    jrelay(dev(3, 1, 0), ())
    xsend_some(15)
    jrelay(dev(2, 0, 0), ())
    jrelay(dev(2, 1, 0), ())

    def prepare(q, _):
        for zz in range(2):
            a = q * 4 + zz * 2 + lax.rem(c + 1, 2)
            jcopy(0, a, (grp, twin)).wait_recv()
        base = pl.multiple_of(q * chunk, 128)
        here = pl.ds(base, chunk)
        for m in range(chunk // 128):
            part = pl.ds(pl.multiple_of(base + m * 128, 128), 128)
            hi, lo = split(jblock[part, :])
            jhi[part, :] = hi
            jlo[part, :] = lo
        for n in range(occ_block * n_vir // 128):
            hi, lo = split(jblock[here, n * 128:(n + 1) * 128].T)
            jthi[q, n * 128:(n + 1) * 128, :] = hi
            jtlo[q, n * 128:(n + 1) * 128, :] = lo
        return 0

    lax.fori_loop(0, 4, prepare, 0)

    def half(k, _):
        acc[...] = jnp.zeros_like(acc)

        def first(q, _):
            for m in range(4):
                a = q * 4 + m

                @pl.when(a != me)
                def _():
                    xcopy(k, 0, a, twin).wait_recv()
            for m in range(4):
                hi, lo = split(held[k, rows(q * 4 + m), :])
                xhi[m * depth:(m + 1) * depth, :] = hi
                xlo[m * depth:(m + 1) * depth, :] = lo
            acc[...] += jnp.dot(jthi[q], xhi[...], preferred_element_type=jnp.float32)
            acc[...] += jnp.dot(jthi[q], xlo[...], preferred_element_type=jnp.float32)
            acc[...] += jnp.dot(jtlo[q], xhi[...], preferred_element_type=jnp.float32)
            return 0

        lax.fori_loop(0, 4, first, 0)
        level_i = occ[order[grp * n_occ + me * occ_block + k]]

        def amplitude(j, _):
            level_j = occ[order[prv * n_occ + owners[0, grp] * occ_block + j]]
            shift = level_shift - level_i - level_j
            for b in range(n_vir // 128):
                for a in range(n_vir // 128):
                    one = acc[pl.ds(pl.multiple_of(j * n_vir + b * 128, 128), 128), a * 128:(a + 1) * 128]
                    two = acc[pl.ds(pl.multiple_of(j * n_vir + a * 128, 128), 128), b * 128:(b + 1) * 128]
                    gap = vsum[b * 128:(b + 1) * 128, a * 128:(a + 1) * 128] + shift
                    hi, lo = split((2.0 * one - two.T) / gap)
                    at = pl.ds(pl.multiple_of(j * n_vir + b * 128, 128), 128)
                    ahi[at, a * 128:(a + 1) * 128] = hi
                    alo[at, a * 128:(a + 1) * 128] = lo
            return 0

        lax.fori_loop(0, occ_block, amplitude, 0)

        def second(q, _):
            here = pl.ds(pl.multiple_of(q * chunk, 128), chunk)
            part = jnp.dot(jhi[here, :], ahi[...], preferred_element_type=jnp.float32)
            part += jnp.dot(jhi[here, :], alo[...], preferred_element_type=jnp.float32)
            part += jnp.dot(jlo[here, :], ahi[...], preferred_element_type=jnp.float32)
            dens[k, here, :] = part
            return 0

        lax.fori_loop(0, 4, second, 0)
        back[k, rows(me), :] = dens[k, rows(me), :]
        for n, step in enumerate(ROUTE):
            ocopy(k, n, me, dev(*step)).start()
        return 0

    lax.fori_loop(0, occ_block, half, 0)

    for k in range(occ_block):
        for a in range(n_aux):
            @pl.when(a != me)
            def _():
                ocopy(k, 0, a, twin).wait_recv()
            for n in lanes:
                out[n, pl.ds(a * occ_block + k, depth, stride=n_occ), :] = back[
                    k, a * depth:(a + 1) * depth, n * 128:(n + 1) * 128]

    jcopy(0, me, (nxt, me), jcut).wait_send()
    for copy in sent:
        copy.wait_send()
    for k in range(occ_block):
        for n, step in enumerate(ROUTE):
            xcopy(k, n, me, dev(*step)).wait_send()
            ocopy(k, n, me, dev(*step)).wait_send()


def body(integrals, occ_energy, vir_energy, orbital_order, owners):
    n_grp = lax.axis_size("grp")
    n_aux = lax.axis_size("aux")
    depth, n_occ, n_vir = integrals.shape
    occ_block = n_occ // n_aux
    total = depth * n_aux
    jb = occ_block * n_vir
    f32, bf16 = jnp.float32, jnp.bfloat16
    sizes = (n_grp, n_aux, depth, n_occ, n_vir, occ_block)
    smem = pl.BlockSpec(memory_space=pltpu.SMEM)
    vmem = pl.BlockSpec(memory_space=pltpu.VMEM)
    out = pl.pallas_call(
        lambda *refs: kernel(sizes, *refs),
        out_shape=jax.ShapeDtypeStruct((n_vir // 128, depth * n_occ, 128), f32),
        in_specs=[smem, smem, smem, vmem, pl.BlockSpec(memory_space=pl.ANY)],
        out_specs=vmem,
        scratch_shapes=[
            pltpu.VMEM((n_vir // 128, depth * n_occ, 128), f32),
            pltpu.VMEM((occ_block, total, n_vir), f32),
            pltpu.VMEM((occ_block, total, n_vir), f32),
            pltpu.VMEM((total, jb), f32),
            pltpu.VMEM((depth, jb), f32),
            pltpu.VMEM((total, jb), bf16),
            pltpu.VMEM((total, jb), bf16),
            pltpu.VMEM((4, jb, 4 * depth), bf16),
            pltpu.VMEM((4, jb, 4 * depth), bf16),
            pltpu.VMEM((4 * depth, n_vir), bf16),
            pltpu.VMEM((4 * depth, n_vir), bf16),
            pltpu.VMEM((jb, n_vir), f32),
            pltpu.VMEM((jb, n_vir), bf16),
            pltpu.VMEM((jb, n_vir), bf16),
            pltpu.VMEM((n_vir, n_vir), f32),
            pltpu.VMEM((occ_block, total, n_vir), f32),
            pltpu.VMEM((occ_block, total, n_vir), f32),
            pltpu.SemaphoreType.DMA((n_vir // 128,)),
            pltpu.SemaphoreType.DMA((24,)),
            pltpu.SemaphoreType.DMA((n_aux,)),
            pltpu.SemaphoreType.DMA((occ_block, n_aux)),
            pltpu.SemaphoreType.DMA((occ_block, n_aux)),
            pltpu.SemaphoreType.DMA((occ_block, n_aux)),
            pltpu.SemaphoreType.DMA((occ_block, n_aux)),
        ],
        compiler_params=pltpu.CompilerParams(
            collective_id=0, has_side_effects=True, vmem_limit_bytes=63 << 20),
    )(occ_energy, orbital_order, owners, vir_energy.reshape(1, n_vir), integrals.reshape(depth * n_occ, n_vir))
    return jnp.swapaxes(out, 0, 1).reshape(depth, n_occ, n_vir)


def solution(mesh):
    in_specs = (P("aux", "grp", None), P(), P(), P(), P())
    out_specs = P("aux", "grp", None)
    return jax.shard_map(body, mesh=mesh, in_specs=in_specs, out_specs=out_specs, check_vma=False)
```

```python
import jax
import jax.numpy as jnp
from jax import lax
from jax.experimental import pallas as pl
from jax.experimental.pallas import tpu as pltpu
from jax.sharding import PartitionSpec as P

level_shift = 0.5
MESH = pl.DeviceIdType.MESH

PIECES = 3

ROUTE = (
    (1, 0, 0), (3, 1, 0), (2, 1, 0), (0, 1, 0), (2, 0, 0),
    (1, 1, 0), (3, 0, 0), (0, 0, 1), (1, 0, 1), (3, 1, 1),
    (2, 1, 1), (0, 1, 1), (2, 0, 1), (1, 1, 1), (3, 0, 1),
)


def split(x):
    hi = x.astype(jnp.bfloat16)
    lo = (x - hi.astype(jnp.float32)).astype(jnp.bfloat16)
    return hi, lo


def kernel(sizes, occ, order, owners, vir, in_hbm, out, rows_in, staged, held, jblock, jcut, jhi, jlo,
           jthi, jtlo, xhi, xlo, acc, ahi, alo, vsum, dens, back, load_sem, jsend, jrecv, xsend, xrecv,
           osend, orecv):
    n_grp, n_aux, depth, n_occ, n_vir, occ_block = sizes
    chunk = 4 * depth
    grp = lax.axis_index("grp")
    me = lax.axis_index("aux")
    y, z, c = lax.div(me, 4), lax.rem(lax.div(me, 2), 2), lax.rem(me, 2)
    nxt = lax.rem(grp + 1, n_grp)
    prv = lax.rem(grp + n_grp - 1, n_grp)

    def dev(dy, dz, dc):
        return lax.rem(y + dy, 4) * 4 + lax.rem(z + dz, 2) * 2 + lax.rem(c + dc, 2)

    def rows(a):
        return pl.ds(pl.multiple_of(a * depth, 8), depth)

    lanes = range(n_vir // 128)
    loads = [pltpu.make_async_copy(in_hbm.at[:, n * 128:(n + 1) * 128], rows_in.at[n], load_sem.at[n]) for n in lanes]
    for load in loads:
        load.start()
    barrier = pltpu.get_barrier_semaphore()
    for n in range(1, 16):
        pl.semaphore_signal(barrier, inc=1, device_id=(grp, lax.rem(me + n, 16)), device_id_type=MESH)
    pl.semaphore_signal(barrier, inc=1, device_id=(nxt, me), device_id_type=MESH)
    pl.semaphore_signal(barrier, inc=1, device_id=(prv, me), device_id_type=MESH)

    wide = jnp.broadcast_to(vir[...][None, :], (n_vir, n_vir))
    vsum[...] = wide + wide.T
    for load in loads:
        load.wait()

    picked = owners[0, nxt] * occ_block
    for k in range(occ_block):
        for n in lanes:
            at = k * n_vir + n * 128
            jcut[:, at:at + 128] = rows_in[n, pl.ds(picked + k, depth, stride=n_occ), :]
    pl.semaphore_wait(barrier, 17)

    piece = depth // PIECES

    def jcopy(n, p, a, target, src=None):
        at = pl.ds(pl.multiple_of(a * depth + p * piece, 8), piece)
        return pltpu.make_async_remote_copy(
            src_ref=jblock.at[at, :] if src is None else src, dst_ref=jblock.at[at, :],
            send_sem=jsend.at[n], recv_sem=jrecv.at[p, a], device_id=target, device_id_type=MESH)

    hops = [jcopy(p, p, me, (nxt, me), jcut.at[p * piece:(p + 1) * piece, :]) for p in range(PIECES)]
    for hop in hops:
        hop.start()

    def xcopy(k, n, a, target):
        return pltpu.make_async_remote_copy(
            src_ref=staged.at[k, rows(target), :], dst_ref=held.at[k, rows(a), :],
            send_sem=xsend.at[k, n], recv_sem=xrecv.at[k, a], device_id=(grp, target), device_id_type=MESH)

    def ocopy(k, n, a, target):
        return pltpu.make_async_remote_copy(
            src_ref=dens.at[k, rows(target), :], dst_ref=back.at[k, rows(a), :],
            send_sem=osend.at[k, n], recv_sem=orecv.at[k, a], device_id=(grp, target), device_id_type=MESH)

    xorder = [(k, n) for k in range(occ_block) for n in range(len(ROUTE))]

    def xsend_some(first, last):
        for k, n in xorder[first:last]:
            xcopy(k, n, me, dev(*ROUTE[n])).start()

    up, down, over, twin = dev(1, 0, 0), dev(3, 0, 0), dev(0, 1, 0), dev(0, 0, 1)
    across, beyond, far = dev(1, 1, 0), dev(2, 0, 0), dev(2, 1, 0)
    behind = dev(3, 1, 0)
    by_y = ((me, (up, down, over)), (over, (up, down)), (down, (up,)), (across, (down,)),
            (up, ()), (behind, ()), (beyond, ()), (far, ()))
    by_z = ((me, (up, down, over)), (down, (over, up)), (up, (over,)), (across, (down,)),
            (over, ()), (behind, ()), (beyond, ()), (far, ()))
    plans = (by_z, by_y, by_z)
    sent = []

    def jrelay(p, event):
        a, targets = plans[p][event]
        jcopy(0, p, a, (grp, twin)).wait_recv()
        for t in targets + (twin,):
            copy = jcopy(len(sent) + PIECES, p, a, (grp, t))
            copy.start()
            sent.append(copy)

    for p, event in ((0, 0), (1, 0), (0, 1), (0, 2), (2, 0), (1, 1), (1, 2), (0, 3), (2, 1), (2, 2), (1, 3), (2, 3)):
        jrelay(p, event)
    for d in range(n_aux):
        for k in range(occ_block):
            for n in lanes:
                staged[k, d * depth:(d + 1) * depth, n * 128:(n + 1) * 128] = rows_in[
                    n, pl.ds(d * occ_block + k, depth, stride=n_occ), :]
    for k in range(occ_block):
        held[k, rows(me), :] = staged[k, rows(me), :]

    xsend_some(0, 30)
    for event in range(4, 8):
        for p in range(PIECES):
            jrelay(p, event)

    def prepare(q, _):
        for zz in range(2):
            a = q * 4 + zz * 2 + lax.rem(c + 1, 2)
            for p in range(PIECES):
                jcopy(0, p, a, (grp, twin)).wait_recv()
        base = pl.multiple_of(q * chunk, 128)
        here = pl.ds(base, chunk)
        for m in range(chunk // 128):
            part = pl.ds(pl.multiple_of(base + m * 128, 128), 128)
            hi, lo = split(jblock[part, :])
            jhi[part, :] = hi
            jlo[part, :] = lo
        for n in range(occ_block * n_vir // 128):
            hi, lo = split(jblock[here, n * 128:(n + 1) * 128].T)
            jthi[q, n * 128:(n + 1) * 128, :] = hi
            jtlo[q, n * 128:(n + 1) * 128, :] = lo
        return 0

    lax.fori_loop(0, 4, prepare, 0)

    def half(k, _):
        acc[...] = jnp.zeros_like(acc)

        def first(q, _):
            for m in range(4):
                a = q * 4 + m

                @pl.when(a != me)
                def _():
                    xcopy(k, 0, a, twin).wait_recv()
            for m in range(4):
                hi, lo = split(held[k, rows(q * 4 + m), :])
                xhi[m * depth:(m + 1) * depth, :] = hi
                xlo[m * depth:(m + 1) * depth, :] = lo
            acc[...] += jnp.dot(jthi[q], xhi[...], preferred_element_type=jnp.float32)
            acc[...] += jnp.dot(jthi[q], xlo[...], preferred_element_type=jnp.float32)
            acc[...] += jnp.dot(jtlo[q], xhi[...], preferred_element_type=jnp.float32)
            return 0

        lax.fori_loop(0, 4, first, 0)
        level_i = occ[order[grp * n_occ + me * occ_block + k]]

        def amplitude(j, _):
            level_j = occ[order[prv * n_occ + owners[0, grp] * occ_block + j]]
            shift = level_shift - level_i - level_j
            for b in range(n_vir // 128):
                for a in range(n_vir // 128):
                    one = acc[pl.ds(pl.multiple_of(j * n_vir + b * 128, 128), 128), a * 128:(a + 1) * 128]
                    two = acc[pl.ds(pl.multiple_of(j * n_vir + a * 128, 128), 128), b * 128:(b + 1) * 128]
                    gap = vsum[b * 128:(b + 1) * 128, a * 128:(a + 1) * 128] + shift
                    hi, lo = split((2.0 * one - two.T) / gap)
                    at = pl.ds(pl.multiple_of(j * n_vir + b * 128, 128), 128)
                    ahi[at, a * 128:(a + 1) * 128] = hi
                    alo[at, a * 128:(a + 1) * 128] = lo
            return 0

        lax.fori_loop(0, occ_block, amplitude, 0)

        def second(q, _):
            here = pl.ds(pl.multiple_of(q * chunk, 128), chunk)
            part = jnp.dot(jhi[here, :], ahi[...], preferred_element_type=jnp.float32)
            part += jnp.dot(jhi[here, :], alo[...], preferred_element_type=jnp.float32)
            part += jnp.dot(jlo[here, :], ahi[...], preferred_element_type=jnp.float32)
            dens[k, here, :] = part
            return 0

        lax.fori_loop(0, 4, second, 0)
        back[k, rows(me), :] = dens[k, rows(me), :]
        for n, step in enumerate(ROUTE):
            ocopy(k, n, me, dev(*step)).start()
        return 0

    lax.fori_loop(0, occ_block, half, 0)

    for k in range(occ_block):
        for a in range(n_aux):
            @pl.when(a != me)
            def _():
                ocopy(k, 0, a, twin).wait_recv()
            for n in lanes:
                out[n, pl.ds(a * occ_block + k, depth, stride=n_occ), :] = back[
                    k, a * depth:(a + 1) * depth, n * 128:(n + 1) * 128]

    for copy in hops + sent:
        copy.wait_send()
    for k in range(occ_block):
        for n, step in enumerate(ROUTE):
            xcopy(k, n, me, dev(*step)).wait_send()
            ocopy(k, n, me, dev(*step)).wait_send()


def write(parts, held, out, sem):
    lanes, count, _ = held.shape
    step = count // parts
    copies = []
    for p in range(parts):
        for n in range(lanes):
            at = pl.ds(p * step, step)
            copies.append(pltpu.make_async_copy(held.at[n, at, :], out.at[at, n * 128:(n + 1) * 128], sem.at[p, n]))
            copies[-1].start()
    for copy in copies:
        copy.wait()


def body(integrals, occ_energy, vir_energy, orbital_order, owners):
    n_grp = lax.axis_size("grp")
    n_aux = lax.axis_size("aux")
    depth, n_occ, n_vir = integrals.shape
    occ_block = n_occ // n_aux
    total = depth * n_aux
    jb = occ_block * n_vir
    f32, bf16 = jnp.float32, jnp.bfloat16
    sizes = (n_grp, n_aux, depth, n_occ, n_vir, occ_block)
    smem = pl.BlockSpec(memory_space=pltpu.SMEM)
    vmem = pl.BlockSpec(memory_space=pltpu.VMEM)
    out = pl.pallas_call(
        lambda *refs: kernel(sizes, *refs),
        out_shape=pltpu.VMEM((n_vir // 128, depth * n_occ, 128), f32),
        in_specs=[smem, smem, smem, vmem, pl.BlockSpec(memory_space=pl.ANY)],
        out_specs=vmem,
        scratch_shapes=[
            pltpu.VMEM((n_vir // 128, depth * n_occ, 128), f32),
            pltpu.VMEM((occ_block, total, n_vir), f32),
            pltpu.VMEM((occ_block, total, n_vir), f32),
            pltpu.VMEM((total, jb), f32),
            pltpu.VMEM((depth, jb), f32),
            pltpu.VMEM((total, jb), bf16),
            pltpu.VMEM((total, jb), bf16),
            pltpu.VMEM((4, jb, 4 * depth), bf16),
            pltpu.VMEM((4, jb, 4 * depth), bf16),
            pltpu.VMEM((4 * depth, n_vir), bf16),
            pltpu.VMEM((4 * depth, n_vir), bf16),
            pltpu.VMEM((jb, n_vir), f32),
            pltpu.VMEM((jb, n_vir), bf16),
            pltpu.VMEM((jb, n_vir), bf16),
            pltpu.VMEM((n_vir, n_vir), f32),
            pltpu.VMEM((occ_block, total, n_vir), f32),
            pltpu.VMEM((occ_block, total, n_vir), f32),
            pltpu.SemaphoreType.DMA((n_vir // 128,)),
            pltpu.SemaphoreType.DMA((PIECES * 16,)),
            pltpu.SemaphoreType.DMA((PIECES, n_aux)),
            pltpu.SemaphoreType.DMA((occ_block, n_aux)),
            pltpu.SemaphoreType.DMA((occ_block, n_aux)),
            pltpu.SemaphoreType.DMA((occ_block, n_aux)),
            pltpu.SemaphoreType.DMA((occ_block, n_aux)),
        ],
        compiler_params=pltpu.CompilerParams(
            collective_id=0, has_side_effects=True, vmem_limit_bytes=50 << 20),
    )(occ_energy, orbital_order, owners, vir_energy, integrals.reshape(depth * n_occ, n_vir))
    parts = 4
    out = pl.pallas_call(
        lambda *refs: write(parts, *refs),
        out_shape=jax.ShapeDtypeStruct((depth * n_occ, n_vir), f32),
        in_specs=[vmem],
        out_specs=pl.BlockSpec(memory_space=pl.ANY),
        scratch_shapes=[pltpu.SemaphoreType.DMA((parts, n_vir // 128))],
        compiler_params=pltpu.CompilerParams(vmem_limit_bytes=8 << 20),
    )(out)
    return out.reshape(depth, n_occ, n_vir)


def solution(mesh):
    in_specs = (P("aux", "grp", None), P(), P(), P(), P())
    out_specs = P("aux", "grp", None)
    return jax.shard_map(body, mesh=mesh, in_specs=in_specs, out_specs=out_specs, check_vma=False)
```

```python
import jax
import jax.numpy as jnp
from jax import lax
from jax.experimental import pallas as pl
from jax.experimental.pallas import tpu as pltpu
from jax.sharding import PartitionSpec as P

level_shift = 0.5
MESH = pl.DeviceIdType.MESH

PIECES = 3

EVENTS = ((0, 0), (1, 0), (0, 1), (0, 2), (2, 0), (1, 1), (1, 2), (0, 3), (2, 1), (2, 2), (1, 3), (2, 3))
EARLY = (0, 6, 3)
FILL = (6, 0, 0, 0, 0, 0, 0, 0, 0, 0, 6, 0, 0)
FIRST = 3
STAGE = (0, 0, 0, 0, 0, 12, 0, 0, 0, 0, 0, 0, 0)

PARTS = 2

ROUTE = (
    (1, 0, 0), (3, 1, 0), (2, 1, 0), (0, 1, 0), (2, 0, 0),
    (1, 1, 0), (3, 0, 0), (0, 0, 1), (1, 0, 1), (3, 1, 1),
    (2, 1, 1), (0, 1, 1), (2, 0, 1), (1, 1, 1), (3, 0, 1),
)


def split(x):
    hi = x.astype(jnp.bfloat16)
    lo = (x - hi.astype(jnp.float32)).astype(jnp.bfloat16)
    return hi, lo


def kernel(sizes, occ, order, owners, vir, in_hbm, out, rows_in, staged, held, jblock, jcut, jhi, jlo,
           jthi, jtlo, xhi, xlo, acc, ahi, alo, vsum, dens, back, load_sem, jsend, jrecv, xsend, xrecv,
           osend, orecv):
    n_grp, n_aux, depth, n_occ, n_vir, occ_block = sizes
    chunk = 4 * depth
    grp = lax.axis_index("grp")
    me = lax.axis_index("aux")
    y, z, c = lax.div(me, 4), lax.rem(lax.div(me, 2), 2), lax.rem(me, 2)
    nxt = lax.rem(grp + 1, n_grp)
    prv = lax.rem(grp + n_grp - 1, n_grp)

    def dev(dy, dz, dc):
        return lax.rem(y + dy, 4) * 4 + lax.rem(z + dz, 2) * 2 + lax.rem(c + dc, 2)

    def swap(group):
        return 1 - jnp.minimum(lax.rem(group, 4), 1)

    def shard(dy, dz, dc):
        return dev(dy, dz + swap(grp), dc)

    def rows(a):
        return pl.ds(pl.multiple_of(a * depth, 8), depth)

    lanes = range(n_vir // 128)
    loads = [pltpu.make_async_copy(in_hbm.at[:, n * 128:(n + 1) * 128], rows_in.at[n], load_sem.at[n]) for n in lanes]
    for load in loads:
        load.start()
    barrier = pltpu.get_barrier_semaphore()
    for n in range(1, 16):
        pl.semaphore_signal(barrier, inc=1, device_id=(grp, lax.rem(me + n, 16)), device_id_type=MESH)
    pl.semaphore_signal(barrier, inc=1, device_id=(nxt, dev(0, swap(nxt), 0)), device_id_type=MESH)
    pl.semaphore_signal(barrier, inc=1, device_id=(prv, shard(0, 0, 0)), device_id_type=MESH)

    wide = jnp.broadcast_to(vir[...][None, :], (n_vir, n_vir))
    vsum[...] = wide + wide.T
    for load in loads:
        load.wait()

    picked = owners[0, nxt] * occ_block
    for k in range(occ_block):
        for n in lanes:
            at = k * n_vir + n * 128
            jcut[:, at:at + 128] = rows_in[n, pl.ds(picked + k, depth, stride=n_occ), :]

    piece = depth // PIECES

    def jcopy(n, p, a, target, src=None):
        at = pl.ds(pl.multiple_of(a * depth + p * piece, 8), piece)
        return pltpu.make_async_remote_copy(
            src_ref=jblock.at[at, :] if src is None else src, dst_ref=jblock.at[at, :],
            send_sem=jsend.at[n], recv_sem=jrecv.at[p, a], device_id=target, device_id_type=MESH)

    def part(a, h):
        size = depth // PARTS
        return rows(a) if h is None else pl.ds(pl.multiple_of(a * depth + h * size, 8), size)

    def xcopy(k, n, a, target, h=None):
        return pltpu.make_async_remote_copy(
            src_ref=staged.at[k, part(target, h), :], dst_ref=held.at[k, part(a, h), :],
            send_sem=xsend.at[k, n], recv_sem=xrecv.at[k, a], device_id=(grp, target), device_id_type=MESH)

    def ocopy(k, n, a, target, h=None):
        return pltpu.make_async_remote_copy(
            src_ref=dens.at[k, part(target, h), :], dst_ref=back.at[k, part(a, h), :],
            send_sem=osend.at[k, n], recv_sem=orecv.at[k, a], device_id=(grp, target), device_id_type=MESH)

    def stage(k, a):
        for n in lanes:
            staged[k, rows(a), n * 128:(n + 1) * 128] = rows_in[n, pl.ds(a * occ_block + k, depth, stride=n_occ), :]

    first = [(0, n, h) for h in range(PARTS) for n in EARLY]
    xorder = first + [e for e in [(k, n, h) for k in range(occ_block) for h in range(PARTS) for n in range(15)]
                      if e not in first]
    blocks = [(0, n) for n in EARLY] + [(0, n) for n in range(15) if n not in EARLY] + [(1, n) for n in range(15)]
    done = [0]
    ready = [0]

    def xstage(count):
        for k, n in blocks[ready[0]:ready[0] + count]:
            stage(k, dev(*ROUTE[n]))
        ready[0] += count

    def xsend_some(count):
        for k, n, h in xorder[done[0]:done[0] + count]:
            xcopy(k, n, me, dev(*ROUTE[n]), h).start()
        done[0] += count

    xstage(FIRST)
    pl.semaphore_wait(barrier, 17)
    hops = [jcopy(p, p, me, (nxt, dev(0, swap(nxt), 0)), jcut.at[p * piece:(p + 1) * piece, :]) for p in range(PIECES)]
    for hop in hops:
        hop.start()

    up, down, over, twin = dev(1, 0, 0), dev(3, 0, 0), dev(0, 1, 0), dev(0, 0, 1)
    own = (shard(0, 0, 0), (up, down, over))
    opposite, above, below, across = shard(0, 1, 0), shard(1, 0, 0), shard(3, 0, 0), shard(1, 1, 0)
    rest = ((shard(3, 1, 0), ()), (shard(2, 0, 0), ()), (shard(2, 1, 0), ()))
    by_y = (own, (opposite, (up, down)), (below, (up,)), (across, (down,)), (above, ())) + rest
    by_z = (own, (below, (over, up)), (above, (over,)), (across, (down,)), (opposite, ())) + rest
    plans = (by_z, by_y, by_z)
    sent = []

    def jrelay(p, event):
        a, targets = plans[p][event]
        jcopy(0, p, a, (grp, twin)).wait_recv()
        for t in targets + (twin,):
            copy = jcopy(len(sent) + PIECES, p, a, (grp, t))
            copy.start()
            sent.append(copy)

    xsend_some(FILL[0])
    xstage(STAGE[0])
    for at, (p, event) in enumerate(EVENTS):
        jrelay(p, event)
        xsend_some(FILL[at + 1])
        xstage(STAGE[at + 1])
    xsend_some(15 * PARTS - done[0])
    xstage(30 - ready[0])
    xsend_some(30 * PARTS - done[0])
    for k in range(occ_block):
        for n in lanes:
            held[k, rows(me), n * 128:(n + 1) * 128] = rows_in[
                n, pl.ds(me * occ_block + k, depth, stride=n_occ), :]
    for event in range(4, 8):
        for p in range(PIECES):
            jrelay(p, event)

    def prepare(q, _):
        for zz in range(2):
            a = q * 4 + zz * 2 + lax.rem(c + 1, 2)
            for p in range(PIECES):
                jcopy(0, p, a, (grp, twin)).wait_recv()
        base = pl.multiple_of(q * chunk, 128)
        here = pl.ds(base, chunk)
        for m in range(chunk // 128):
            part = pl.ds(pl.multiple_of(base + m * 128, 128), 128)
            hi, lo = split(jblock[part, :])
            jhi[part, :] = hi
            jlo[part, :] = lo
        for n in range(occ_block * n_vir // 128):
            hi, lo = split(jblock[here, n * 128:(n + 1) * 128].T)
            jthi[q, n * 128:(n + 1) * 128, :] = hi
            jtlo[q, n * 128:(n + 1) * 128, :] = lo
        return 0

    lax.fori_loop(0, 4, prepare, 0)

    def half(k, _):
        acc[...] = jnp.zeros_like(acc)

        def first(q, _):
            for m in range(4):
                a = q * 4 + m

                @pl.when(a != me)
                def _():
                    xcopy(k, 0, a, twin).wait_recv()
            for m in range(4):
                hi, lo = split(held[k, rows(q * 4 + m), :])
                xhi[m * depth:(m + 1) * depth, :] = hi
                xlo[m * depth:(m + 1) * depth, :] = lo
            acc[...] += jnp.dot(jthi[q], xhi[...], preferred_element_type=jnp.float32)
            acc[...] += jnp.dot(jthi[q], xlo[...], preferred_element_type=jnp.float32)
            acc[...] += jnp.dot(jtlo[q], xhi[...], preferred_element_type=jnp.float32)
            return 0

        lax.fori_loop(0, 4, first, 0)
        level_i = occ[order[grp * n_occ + me * occ_block + k]]

        def amplitude(j, _):
            level_j = occ[order[prv * n_occ + owners[0, grp] * occ_block + j]]
            shift = level_shift - level_i - level_j
            for b in range(n_vir // 128):
                for a in range(n_vir // 128):
                    one = acc[pl.ds(pl.multiple_of(j * n_vir + b * 128, 128), 128), a * 128:(a + 1) * 128]
                    two = acc[pl.ds(pl.multiple_of(j * n_vir + a * 128, 128), 128), b * 128:(b + 1) * 128]
                    gap = vsum[b * 128:(b + 1) * 128, a * 128:(a + 1) * 128] + shift
                    hi, lo = split((2.0 * one - two.T) / gap)
                    at = pl.ds(pl.multiple_of(j * n_vir + b * 128, 128), 128)
                    ahi[at, a * 128:(a + 1) * 128] = hi
                    alo[at, a * 128:(a + 1) * 128] = lo
            return 0

        lax.fori_loop(0, occ_block, amplitude, 0)

        def second(q, _):
            here = pl.ds(pl.multiple_of(q * chunk, 128), chunk)
            part = jnp.dot(jhi[here, :], ahi[...], preferred_element_type=jnp.float32)
            part += jnp.dot(jhi[here, :], alo[...], preferred_element_type=jnp.float32)
            part += jnp.dot(jlo[here, :], ahi[...], preferred_element_type=jnp.float32)
            dens[k, here, :] = part
            return 0

        lax.fori_loop(0, 4, second, 0)
        back[k, rows(me), :] = dens[k, rows(me), :]
        for h in range(PARTS):
            for n, step in enumerate(ROUTE):
                ocopy(k, n, me, dev(*step), h).start()
        return 0

    lax.fori_loop(0, occ_block, half, 0)

    for k in range(occ_block):
        for a in range(n_aux):
            @pl.when(a != me)
            def _():
                ocopy(k, 0, a, twin).wait_recv()
            for n in lanes:
                out[n, pl.ds(a * occ_block + k, depth, stride=n_occ), :] = back[
                    k, a * depth:(a + 1) * depth, n * 128:(n + 1) * 128]

    for copy in hops + sent:
        copy.wait_send()
    for k in range(occ_block):
        for n, step in enumerate(ROUTE):
            xcopy(k, n, me, dev(*step)).wait_send()
            ocopy(k, n, me, dev(*step)).wait_send()


def write(parts, held, out, sem):
    lanes, count, _ = held.shape
    step = count // parts
    copies = []
    for p in range(parts):
        for n in range(lanes):
            at = pl.ds(p * step, step)
            copies.append(pltpu.make_async_copy(held.at[n, at, :], out.at[at, n * 128:(n + 1) * 128], sem.at[p, n]))
            copies[-1].start()
    for copy in copies:
        copy.wait()


def body(integrals, occ_energy, vir_energy, orbital_order, owners):
    n_grp = lax.axis_size("grp")
    n_aux = lax.axis_size("aux")
    depth, n_occ, n_vir = integrals.shape
    occ_block = n_occ // n_aux
    total = depth * n_aux
    jb = occ_block * n_vir
    f32, bf16 = jnp.float32, jnp.bfloat16
    sizes = (n_grp, n_aux, depth, n_occ, n_vir, occ_block)
    smem = pl.BlockSpec(memory_space=pltpu.SMEM)
    vmem = pl.BlockSpec(memory_space=pltpu.VMEM)
    out = pl.pallas_call(
        lambda *refs: kernel(sizes, *refs),
        out_shape=pltpu.VMEM((n_vir // 128, depth * n_occ, 128), f32),
        in_specs=[smem, smem, smem, vmem, pl.BlockSpec(memory_space=pl.ANY)],
        out_specs=vmem,
        scratch_shapes=[
            pltpu.VMEM((n_vir // 128, depth * n_occ, 128), f32),
            pltpu.VMEM((occ_block, total, n_vir), f32),
            pltpu.VMEM((occ_block, total, n_vir), f32),
            pltpu.VMEM((total, jb), f32),
            pltpu.VMEM((depth, jb), f32),
            pltpu.VMEM((total, jb), bf16),
            pltpu.VMEM((total, jb), bf16),
            pltpu.VMEM((4, jb, 4 * depth), bf16),
            pltpu.VMEM((4, jb, 4 * depth), bf16),
            pltpu.VMEM((4 * depth, n_vir), bf16),
            pltpu.VMEM((4 * depth, n_vir), bf16),
            pltpu.VMEM((jb, n_vir), f32),
            pltpu.VMEM((jb, n_vir), bf16),
            pltpu.VMEM((jb, n_vir), bf16),
            pltpu.VMEM((n_vir, n_vir), f32),
            pltpu.VMEM((occ_block, total, n_vir), f32),
            pltpu.VMEM((occ_block, total, n_vir), f32),
            pltpu.SemaphoreType.DMA((n_vir // 128,)),
            pltpu.SemaphoreType.DMA((PIECES * 16,)),
            pltpu.SemaphoreType.DMA((PIECES, n_aux)),
            pltpu.SemaphoreType.DMA((occ_block, n_aux)),
            pltpu.SemaphoreType.DMA((occ_block, n_aux)),
            pltpu.SemaphoreType.DMA((occ_block, n_aux)),
            pltpu.SemaphoreType.DMA((occ_block, n_aux)),
        ],
        compiler_params=pltpu.CompilerParams(
            collective_id=0, has_side_effects=True, vmem_limit_bytes=50 << 20),
    )(occ_energy, orbital_order, owners, vir_energy, integrals.reshape(depth * n_occ, n_vir))
    parts = 4
    out = pl.pallas_call(
        lambda *refs: write(parts, *refs),
        out_shape=jax.ShapeDtypeStruct((depth * n_occ, n_vir), f32),
        in_specs=[vmem],
        out_specs=pl.BlockSpec(memory_space=pl.ANY),
        scratch_shapes=[pltpu.SemaphoreType.DMA((parts, n_vir // 128))],
        compiler_params=pltpu.CompilerParams(vmem_limit_bytes=8 << 20),
    )(out)
    return out.reshape(depth, n_occ, n_vir)


def solution(mesh):
    in_specs = (P("aux", "grp", None), P(), P(), P(), P())
    out_specs = P("aux", "grp", None)
    return jax.shard_map(body, mesh=mesh, in_specs=in_specs, out_specs=out_specs, check_vma=False)
```

```python
import jax
import jax.numpy as jnp
from jax import lax
from jax.experimental import pallas as pl
from jax.experimental.pallas import tpu as pltpu
from jax.sharding import PartitionSpec as P

level_shift = 0.5
MESH = pl.DeviceIdType.MESH

PIECES = 6

EVENTS = ((0, 0), (1, 0), (2, 0), (0, 1), (0, 2), (3, 0), (1, 1), (1, 2), (4, 0), (2, 1), (2, 2), (0, 3), (5, 0), (3, 1), (3, 2), (1, 3), (4, 1), (4, 2), (2, 3), (5, 1), (5, 2), (3, 3), (4, 3), (5, 3))
EARLY = (0, 6, 3)
FILL = (9, 0, 0, 0, 0, 0, 0, 0, 0, 0, 0, 0, 0, 0, 0, 0, 0, 0, 0, 0, 0, 9, 0, 0, 0)
FIRST = 3
STAGE = (0, 0, 0, 0, 0, 0, 0, 0, 0, 0, 12, 0, 0, 0, 0, 0, 0, 0, 0, 0, 0, 0, 0, 0, 0)

PARTS = 3

ROUTE = (
    (1, 0, 0), (3, 1, 0), (2, 1, 0), (0, 1, 0), (2, 0, 0),
    (1, 1, 0), (3, 0, 0), (0, 0, 1), (1, 0, 1), (3, 1, 1),
    (2, 1, 1), (0, 1, 1), (2, 0, 1), (1, 1, 1), (3, 0, 1),
)


def split(x):
    hi = x.astype(jnp.bfloat16)
    lo = (x - hi.astype(jnp.float32)).astype(jnp.bfloat16)
    return hi, lo


def kernel(sizes, occ, order, owners, vir, in_hbm, out, rows_in, staged, held, jblock, jcut, jhi, jlo,
           jthi, jtlo, xhi, xlo, acc, ahi, alo, vsum, dens, back, load_sem, jsend, jrecv, xsend, xrecv,
           osend, orecv):
    n_grp, n_aux, depth, n_occ, n_vir, occ_block = sizes
    chunk = 4 * depth
    grp = lax.axis_index("grp")
    me = lax.axis_index("aux")
    y, z, c = lax.div(me, 4), lax.rem(lax.div(me, 2), 2), lax.rem(me, 2)
    nxt = lax.rem(grp + 1, n_grp)
    prv = lax.rem(grp + n_grp - 1, n_grp)

    def dev(dy, dz, dc):
        return lax.rem(y + dy, 4) * 4 + lax.rem(z + dz, 2) * 2 + lax.rem(c + dc, 2)

    def swap(group):
        return 1 - jnp.minimum(lax.rem(group, 4), 1)

    def shard(dy, dz, dc):
        return dev(dy, dz + swap(grp), dc)

    def rows(a):
        return pl.ds(pl.multiple_of(a * depth, 8), depth)

    lanes = range(n_vir // 128)
    loads = [pltpu.make_async_copy(in_hbm.at[:, n * 128:(n + 1) * 128], rows_in.at[n], load_sem.at[n]) for n in lanes]
    for load in loads:
        load.start()
    barrier = pltpu.get_barrier_semaphore()
    for n in range(1, 16):
        pl.semaphore_signal(barrier, inc=1, device_id=(grp, lax.rem(me + n, 16)), device_id_type=MESH)
    pl.semaphore_signal(barrier, inc=1, device_id=(nxt, dev(0, swap(nxt), 0)), device_id_type=MESH)
    pl.semaphore_signal(barrier, inc=1, device_id=(prv, shard(0, 0, 0)), device_id_type=MESH)

    wide = jnp.broadcast_to(vir[...][None, :], (n_vir, n_vir))
    vsum[...] = wide + wide.T
    for load in loads:
        load.wait()

    picked = owners[0, nxt] * occ_block
    for k in range(occ_block):
        for n in lanes:
            at = k * n_vir + n * 128
            jcut[:, at:at + 128] = rows_in[n, pl.ds(picked + k, depth, stride=n_occ), :]

    piece = depth // PIECES

    def jcopy(n, p, a, target, src=None):
        at = pl.ds(pl.multiple_of(a * depth + p * piece, 8), piece)
        return pltpu.make_async_remote_copy(
            src_ref=jblock.at[at, :] if src is None else src, dst_ref=jblock.at[at, :],
            send_sem=jsend.at[n], recv_sem=jrecv.at[p, a], device_id=target, device_id_type=MESH)

    def part(a, h):
        size = depth // PARTS
        return rows(a) if h is None else pl.ds(pl.multiple_of(a * depth + h * size, 8), size)

    def xcopy(k, n, a, target, h=None):
        return pltpu.make_async_remote_copy(
            src_ref=staged.at[k, part(target, h), :], dst_ref=held.at[k, part(a, h), :],
            send_sem=xsend.at[k, n], recv_sem=xrecv.at[k, a], device_id=(grp, target), device_id_type=MESH)

    def ocopy(k, n, a, target, h=None):
        return pltpu.make_async_remote_copy(
            src_ref=dens.at[k, part(target, h), :], dst_ref=back.at[k, part(a, h), :],
            send_sem=osend.at[k, n], recv_sem=orecv.at[k, a], device_id=(grp, target), device_id_type=MESH)

    def stage(k, a):
        for n in lanes:
            staged[k, rows(a), n * 128:(n + 1) * 128] = rows_in[n, pl.ds(a * occ_block + k, depth, stride=n_occ), :]

    first = [(0, n, h) for h in range(PARTS) for n in EARLY]
    xorder = first + [e for e in [(k, n, h) for k in range(occ_block) for h in range(PARTS) for n in range(15)]
                      if e not in first]
    blocks = [(0, n) for n in EARLY] + [(0, n) for n in range(15) if n not in EARLY] + [(1, n) for n in range(15)]
    done = [0]
    ready = [0]

    def xstage(count):
        for k, n in blocks[ready[0]:ready[0] + count]:
            stage(k, dev(*ROUTE[n]))
        ready[0] += count

    def xsend_some(count):
        for k, n, h in xorder[done[0]:done[0] + count]:
            xcopy(k, n, me, dev(*ROUTE[n]), h).start()
        done[0] += count

    xstage(FIRST)
    pl.semaphore_wait(barrier, 17)
    hops = [jcopy(p, p, me, (nxt, dev(0, swap(nxt), 0)), jcut.at[p * piece:(p + 1) * piece, :]) for p in range(PIECES)]
    for hop in hops:
        hop.start()

    up, down, over, twin = dev(1, 0, 0), dev(3, 0, 0), dev(0, 1, 0), dev(0, 0, 1)
    own = (shard(0, 0, 0), (up, down, over))
    opposite, above, below, across = shard(0, 1, 0), shard(1, 0, 0), shard(3, 0, 0), shard(1, 1, 0)
    rest = ((shard(3, 1, 0), ()), (shard(2, 0, 0), ()), (shard(2, 1, 0), ()))
    by_y = (own, (opposite, (up, down)), (below, (up,)), (across, (down,)), (above, ())) + rest
    by_z = (own, (below, (over, up)), (above, (over,)), (across, (down,)), (opposite, ())) + rest
    plans = (by_z, by_y, by_z) * 2
    sent = []

    def jrelay(p, event):
        a, targets = plans[p][event]
        jcopy(0, p, a, (grp, twin)).wait_recv()
        for t in targets + (twin,):
            copy = jcopy(len(sent) + PIECES, p, a, (grp, t))
            copy.start()
            sent.append(copy)

    xsend_some(FILL[0])
    xstage(STAGE[0])
    for at, (p, event) in enumerate(EVENTS):
        jrelay(p, event)
        xsend_some(FILL[at + 1])
        xstage(STAGE[at + 1])
    xsend_some(15 * PARTS - done[0])
    xstage(30 - ready[0])
    xsend_some(30 * PARTS - done[0])
    for k in range(occ_block):
        for n in lanes:
            held[k, rows(me), n * 128:(n + 1) * 128] = rows_in[
                n, pl.ds(me * occ_block + k, depth, stride=n_occ), :]
    for event in range(4, 8):
        for p in range(PIECES):
            jrelay(p, event)

    def prepare(q, _):
        for zz in range(2):
            a = q * 4 + zz * 2 + lax.rem(c + 1, 2)
            for p in range(PIECES):
                jcopy(0, p, a, (grp, twin)).wait_recv()
        base = pl.multiple_of(q * chunk, 128)
        here = pl.ds(base, chunk)
        for m in range(chunk // 128):
            part = pl.ds(pl.multiple_of(base + m * 128, 128), 128)
            hi, lo = split(jblock[part, :])
            jhi[part, :] = hi
            jlo[part, :] = lo
        for n in range(occ_block * n_vir // 128):
            hi, lo = split(jblock[here, n * 128:(n + 1) * 128].T)
            jthi[q, n * 128:(n + 1) * 128, :] = hi
            jtlo[q, n * 128:(n + 1) * 128, :] = lo
        return 0

    lax.fori_loop(0, 4, prepare, 0)

    def half(k, _):
        acc[...] = jnp.zeros_like(acc)

        def first(q, _):
            for m in range(4):
                a = q * 4 + m

                @pl.when(a != me)
                def _():
                    xcopy(k, 0, a, twin).wait_recv()
            for m in range(4):
                hi, lo = split(held[k, rows(q * 4 + m), :])
                xhi[m * depth:(m + 1) * depth, :] = hi
                xlo[m * depth:(m + 1) * depth, :] = lo
            acc[...] += jnp.dot(jthi[q], xhi[...], preferred_element_type=jnp.float32)
            acc[...] += jnp.dot(jthi[q], xlo[...], preferred_element_type=jnp.float32)
            acc[...] += jnp.dot(jtlo[q], xhi[...], preferred_element_type=jnp.float32)
            return 0

        lax.fori_loop(0, 4, first, 0)
        level_i = occ[order[grp * n_occ + me * occ_block + k]]

        def amplitude(j, _):
            level_j = occ[order[prv * n_occ + owners[0, grp] * occ_block + j]]
            shift = level_shift - level_i - level_j
            for b in range(n_vir // 128):
                for a in range(n_vir // 128):
                    one = acc[pl.ds(pl.multiple_of(j * n_vir + b * 128, 128), 128), a * 128:(a + 1) * 128]
                    two = acc[pl.ds(pl.multiple_of(j * n_vir + a * 128, 128), 128), b * 128:(b + 1) * 128]
                    gap = vsum[b * 128:(b + 1) * 128, a * 128:(a + 1) * 128] + shift
                    hi, lo = split((2.0 * one - two.T) / gap)
                    at = pl.ds(pl.multiple_of(j * n_vir + b * 128, 128), 128)
                    ahi[at, a * 128:(a + 1) * 128] = hi
                    alo[at, a * 128:(a + 1) * 128] = lo
            return 0

        lax.fori_loop(0, occ_block, amplitude, 0)

        def second(q, _):
            here = pl.ds(pl.multiple_of(q * chunk, 128), chunk)
            part = jnp.dot(jhi[here, :], ahi[...], preferred_element_type=jnp.float32)
            part += jnp.dot(jhi[here, :], alo[...], preferred_element_type=jnp.float32)
            part += jnp.dot(jlo[here, :], ahi[...], preferred_element_type=jnp.float32)
            dens[k, here, :] = part
            return 0

        lax.fori_loop(0, 4, second, 0)
        back[k, rows(me), :] = dens[k, rows(me), :]
        for h in range(PARTS):
            for n, step in enumerate(ROUTE):
                ocopy(k, n, me, dev(*step), h).start()
        return 0

    lax.fori_loop(0, occ_block, half, 0)

    for k in range(occ_block):
        for dy, dz, dc in ((0, 0, 0),) + ROUTE:
            a = dev(4 - dy, dz, dc)
            if (dy, dz, dc) != (0, 0, 0):
                ocopy(k, 0, a, twin).wait_recv()
            for n in lanes:
                out[n, pl.ds(a * occ_block + k, depth, stride=n_occ), :] = back[k, rows(a), n * 128:(n + 1) * 128]

    for copy in hops + sent:
        copy.wait_send()
    for k in range(occ_block):
        for n, step in enumerate(ROUTE):
            xcopy(k, n, me, dev(*step)).wait_send()
            ocopy(k, n, me, dev(*step)).wait_send()


def write(parts, held, out, sem):
    lanes, count, _ = held.shape
    step = count // parts
    copies = []
    for p in range(parts):
        for n in range(lanes):
            at = pl.ds(p * step, step)
            copies.append(pltpu.make_async_copy(held.at[n, at, :], out.at[at, n * 128:(n + 1) * 128], sem.at[p, n]))
            copies[-1].start()
    for copy in copies:
        copy.wait()


def body(integrals, occ_energy, vir_energy, orbital_order, owners):
    n_grp = lax.axis_size("grp")
    n_aux = lax.axis_size("aux")
    depth, n_occ, n_vir = integrals.shape
    occ_block = n_occ // n_aux
    total = depth * n_aux
    jb = occ_block * n_vir
    f32, bf16 = jnp.float32, jnp.bfloat16
    sizes = (n_grp, n_aux, depth, n_occ, n_vir, occ_block)
    smem = pl.BlockSpec(memory_space=pltpu.SMEM)
    vmem = pl.BlockSpec(memory_space=pltpu.VMEM)
    out = pl.pallas_call(
        lambda *refs: kernel(sizes, *refs),
        out_shape=pltpu.VMEM((n_vir // 128, depth * n_occ, 128), f32),
        in_specs=[smem, smem, smem, vmem, pl.BlockSpec(memory_space=pl.ANY)],
        out_specs=vmem,
        scratch_shapes=[
            pltpu.VMEM((n_vir // 128, depth * n_occ, 128), f32),
            pltpu.VMEM((occ_block, total, n_vir), f32),
            pltpu.VMEM((occ_block, total, n_vir), f32),
            pltpu.VMEM((total, jb), f32),
            pltpu.VMEM((depth, jb), f32),
            pltpu.VMEM((total, jb), bf16),
            pltpu.VMEM((total, jb), bf16),
            pltpu.VMEM((4, jb, 4 * depth), bf16),
            pltpu.VMEM((4, jb, 4 * depth), bf16),
            pltpu.VMEM((4 * depth, n_vir), bf16),
            pltpu.VMEM((4 * depth, n_vir), bf16),
            pltpu.VMEM((jb, n_vir), f32),
            pltpu.VMEM((jb, n_vir), bf16),
            pltpu.VMEM((jb, n_vir), bf16),
            pltpu.VMEM((n_vir, n_vir), f32),
            pltpu.VMEM((occ_block, total, n_vir), f32),
            pltpu.VMEM((occ_block, total, n_vir), f32),
            pltpu.SemaphoreType.DMA((n_vir // 128,)),
            pltpu.SemaphoreType.DMA((PIECES * 16,)),
            pltpu.SemaphoreType.DMA((PIECES, n_aux)),
            pltpu.SemaphoreType.DMA((occ_block, n_aux)),
            pltpu.SemaphoreType.DMA((occ_block, n_aux)),
            pltpu.SemaphoreType.DMA((occ_block, n_aux)),
            pltpu.SemaphoreType.DMA((occ_block, n_aux)),
        ],
        compiler_params=pltpu.CompilerParams(
            collective_id=0, has_side_effects=True, vmem_limit_bytes=50 << 20),
    )(occ_energy, orbital_order, owners, vir_energy, integrals.reshape(depth * n_occ, n_vir))
    parts = 4
    out = pl.pallas_call(
        lambda *refs: write(parts, *refs),
        out_shape=jax.ShapeDtypeStruct((depth * n_occ, n_vir), f32),
        in_specs=[vmem],
        out_specs=pl.BlockSpec(memory_space=pl.ANY),
        scratch_shapes=[pltpu.SemaphoreType.DMA((parts, n_vir // 128))],
        compiler_params=pltpu.CompilerParams(vmem_limit_bytes=8 << 20),
    )(out)
    return out.reshape(depth, n_occ, n_vir)


def solution(mesh):
    in_specs = (P("aux", "grp", None), P(), P(), P(), P())
    out_specs = P("aux", "grp", None)
    return jax.shard_map(body, mesh=mesh, in_specs=in_specs, out_specs=out_specs, check_vma=False)
```

```python
import jax
import jax.numpy as jnp
from jax import lax
from jax.experimental import pallas as pl
from jax.experimental.pallas import tpu as pltpu
from jax.sharding import PartitionSpec as P

level_shift = 0.5
MESH = pl.DeviceIdType.MESH

PIECES = 6

EVENTS = ((0, 0), (1, 0), (2, 0), (0, 1), (0, 2), (3, 0), (1, 1), (1, 2), (4, 0), (2, 1), (2, 2), (0, 3), (5, 0), (3, 1), (3, 2), (1, 3), (4, 1), (4, 2), (2, 3), (5, 1), (5, 2), (3, 3), (4, 3), (5, 3))
AHEAD = 6
AHEAD_STAGE = 10
AHEAD_SEND = 21

EARLY = (0, 6, 3)
FILL = (9, 0, 0, 0, 0, 0, 0, 0, 0, 0, 0, 0, 0, 0, 0, 0, 0, 0, 0, 0, 0, 3, 0, 0, 0)
FIRST = 3
STAGE = (0, 0, 0, 0, 0, 0, 0, 0, 0, 0, 6, 0, 0, 0, 0, 0, 0, 0, 0, 0, 0, 0, 0, 0, 0)

PARTS = 3

ROUTE = (
    (1, 0, 0), (3, 1, 0), (2, 1, 0), (0, 1, 0), (2, 0, 0),
    (1, 1, 0), (3, 0, 0), (0, 0, 1), (1, 0, 1), (3, 1, 1),
    (2, 1, 1), (0, 1, 1), (2, 0, 1), (1, 1, 1), (3, 0, 1),
)


def split(x):
    hi = x.astype(jnp.bfloat16)
    lo = (x - hi.astype(jnp.float32)).astype(jnp.bfloat16)
    return hi, lo


def kernel(sizes, occ, order, owners, vir, in_hbm, out, rows_in, staged, held, jblock, jcut, jhi, jlo,
           jthi, jtlo, xhi, xlo, acc, ahi, alo, vsum, dens, back, load_sem, jsend, jrecv, xsend, xrecv,
           osend, orecv):
    n_grp, n_aux, depth, n_occ, n_vir, occ_block = sizes
    chunk = 4 * depth
    grp = lax.axis_index("grp")
    me = lax.axis_index("aux")
    y, z, c = lax.div(me, 4), lax.rem(lax.div(me, 2), 2), lax.rem(me, 2)
    nxt = lax.rem(grp + 1, n_grp)
    prv = lax.rem(grp + n_grp - 1, n_grp)

    def dev(dy, dz, dc):
        return lax.rem(y + dy, 4) * 4 + lax.rem(z + dz, 2) * 2 + lax.rem(c + dc, 2)

    def swap(group):
        return 1 - jnp.minimum(lax.rem(group, 4), 1)

    def shard(dy, dz, dc):
        return dev(dy, dz + swap(grp), dc)

    def rows(a):
        return pl.ds(pl.multiple_of(a * depth, 8), depth)

    lanes = range(n_vir // 128)
    loads = [pltpu.make_async_copy(in_hbm.at[:, n * 128:(n + 1) * 128], rows_in.at[n], load_sem.at[n]) for n in lanes]
    for load in loads:
        load.start()
    barrier = pltpu.get_barrier_semaphore()
    for n in range(1, 16):
        pl.semaphore_signal(barrier, inc=1, device_id=(grp, lax.rem(me + n, 16)), device_id_type=MESH)
    pl.semaphore_signal(barrier, inc=1, device_id=(nxt, dev(0, swap(nxt), 0)), device_id_type=MESH)
    pl.semaphore_signal(barrier, inc=1, device_id=(prv, shard(0, 0, 0)), device_id_type=MESH)

    wide = jnp.broadcast_to(vir[...][None, :], (n_vir, n_vir))
    vsum[...] = wide + wide.T
    for load in loads:
        load.wait()

    picked = owners[0, nxt] * occ_block
    for k in range(occ_block):
        for n in lanes:
            at = k * n_vir + n * 128
            jcut[:, at:at + 128] = rows_in[n, pl.ds(picked + k, depth, stride=n_occ), :]

    piece = depth // PIECES

    def jcopy(n, p, a, target, src=None):
        at = pl.ds(pl.multiple_of(a * depth + p * piece, 8), piece)
        return pltpu.make_async_remote_copy(
            src_ref=jblock.at[at, :] if src is None else src, dst_ref=jblock.at[at, :],
            send_sem=jsend.at[n], recv_sem=jrecv.at[p, a], device_id=target, device_id_type=MESH)

    def part(a, h):
        size = depth // PARTS
        return rows(a) if h is None else pl.ds(pl.multiple_of(a * depth + h * size, 8), size)

    def xcopy(k, n, a, target, h=None):
        return pltpu.make_async_remote_copy(
            src_ref=staged.at[k, part(target, h), :], dst_ref=held.at[k, part(a, h), :],
            send_sem=xsend.at[k, n], recv_sem=xrecv.at[k, a], device_id=(grp, target), device_id_type=MESH)

    def ocopy(k, n, a, target, h=None):
        return pltpu.make_async_remote_copy(
            src_ref=dens.at[k, part(target, h), :], dst_ref=back.at[k, part(a, h), :],
            send_sem=osend.at[k, n], recv_sem=orecv.at[k, a], device_id=(grp, target), device_id_type=MESH)

    def stage(k, a):
        for n in lanes:
            staged[k, rows(a), n * 128:(n + 1) * 128] = rows_in[n, pl.ds(a * occ_block + k, depth, stride=n_occ), :]

    first = [(0, n, h) for h in range(PARTS) for n in EARLY]
    xorder = first + [e for e in [(k, n, h) for k in range(occ_block) for h in range(PARTS) for n in range(15)]
                      if e not in first]
    blocks = [(0, n) for n in EARLY] + [(0, n) for n in range(15) if n not in EARLY] + [(1, n) for n in range(15)]
    done = [0]
    ready = [0]

    def stage_all(chosen):
        for k, n in chosen:
            stage(k, dev(*ROUTE[n]))

    def send_all(chosen):
        for k, n, h in chosen:
            xcopy(k, n, me, dev(*ROUTE[n]), h).start()

    def xstage(count):
        stage_all(blocks[ready[0]:ready[0] + count])
        ready[0] += count

    def xsend_some(count):
        send_all(xorder[done[0]:done[0] + count])
        done[0] += count

    xstage(FIRST)
    pl.semaphore_wait(barrier, 17)
    hops = [jcopy(p, p, me, (nxt, dev(0, swap(nxt), 0)), jcut.at[p * piece:(p + 1) * piece, :]) for p in range(PIECES)]
    for hop in hops:
        hop.start()

    up, down, over, twin = dev(1, 0, 0), dev(3, 0, 0), dev(0, 1, 0), dev(0, 0, 1)
    own = (shard(0, 0, 0), (up, down, over))
    opposite, above, below, across = shard(0, 1, 0), shard(1, 0, 0), shard(3, 0, 0), shard(1, 1, 0)
    rest = ((shard(3, 1, 0), ()), (shard(2, 0, 0), ()), (shard(2, 1, 0), ()))
    by_y = (own, (opposite, (up, down)), (below, (up,)), (across, (down,)), (above, ())) + rest
    by_z = (own, (below, (over, up)), (above, (over,)), (across, (down,)), (opposite, ())) + rest
    plans = (by_z, by_y, by_z) * 2
    sent = []

    def jrelay(p, event):
        a, targets = plans[p][event]
        jcopy(0, p, a, (grp, twin)).wait_recv()
        for t in targets + (twin,):
            copy = jcopy(len(sent) + PIECES, p, a, (grp, t))
            copy.start()
            sent.append(copy)

    xsend_some(FILL[0])
    xstage(STAGE[0])
    later = (blocks[ready[0]:ready[0] + AHEAD], xorder[done[0]:done[0] + AHEAD])
    ready[0] += AHEAD
    done[0] += AHEAD

    @pl.when(grp == 0)
    def _():
        stage_all(later[0])
        send_all(later[1])

    for at, (p, event) in enumerate(EVENTS):
        jrelay(p, event)
        if at + 1 == AHEAD_STAGE:
            pl.when(grp != 0)(lambda: stage_all(later[0]))
        if at + 1 == AHEAD_SEND:
            pl.when(grp != 0)(lambda: send_all(later[1]))
        xsend_some(FILL[at + 1])
        xstage(STAGE[at + 1])
    xsend_some(15 * PARTS - done[0])
    xstage(30 - ready[0])
    xsend_some(30 * PARTS - done[0])
    for k in range(occ_block):
        for n in lanes:
            held[k, rows(me), n * 128:(n + 1) * 128] = rows_in[
                n, pl.ds(me * occ_block + k, depth, stride=n_occ), :]
    for event in range(4, 8):
        for p in range(PIECES):
            jrelay(p, event)

    def prepare(q, _):
        for zz in range(2):
            a = q * 4 + zz * 2 + lax.rem(c + 1, 2)
            for p in range(PIECES):
                jcopy(0, p, a, (grp, twin)).wait_recv()
        base = pl.multiple_of(q * chunk, 128)
        here = pl.ds(base, chunk)
        for m in range(chunk // 128):
            part = pl.ds(pl.multiple_of(base + m * 128, 128), 128)
            hi, lo = split(jblock[part, :])
            jhi[part, :] = hi
            jlo[part, :] = lo
        for n in range(occ_block * n_vir // 128):
            hi, lo = split(jblock[here, n * 128:(n + 1) * 128].T)
            jthi[q, n * 128:(n + 1) * 128, :] = hi
            jtlo[q, n * 128:(n + 1) * 128, :] = lo
        return 0

    lax.fori_loop(0, 4, prepare, 0)

    def half(k, _):
        acc[...] = jnp.zeros_like(acc)

        def first(q, _):
            for m in range(4):
                a = q * 4 + m

                @pl.when(a != me)
                def _():
                    xcopy(k, 0, a, twin).wait_recv()
            for m in range(4):
                hi, lo = split(held[k, rows(q * 4 + m), :])
                xhi[m * depth:(m + 1) * depth, :] = hi
                xlo[m * depth:(m + 1) * depth, :] = lo
            acc[...] += jnp.dot(jthi[q], xhi[...], preferred_element_type=jnp.float32)
            acc[...] += jnp.dot(jthi[q], xlo[...], preferred_element_type=jnp.float32)
            acc[...] += jnp.dot(jtlo[q], xhi[...], preferred_element_type=jnp.float32)
            return 0

        lax.fori_loop(0, 4, first, 0)
        level_i = occ[order[grp * n_occ + me * occ_block + k]]

        def amplitude(j, _):
            level_j = occ[order[prv * n_occ + owners[0, grp] * occ_block + j]]
            shift = level_shift - level_i - level_j
            for b in range(n_vir // 128):
                for a in range(n_vir // 128):
                    one = acc[pl.ds(pl.multiple_of(j * n_vir + b * 128, 128), 128), a * 128:(a + 1) * 128]
                    two = acc[pl.ds(pl.multiple_of(j * n_vir + a * 128, 128), 128), b * 128:(b + 1) * 128]
                    gap = vsum[b * 128:(b + 1) * 128, a * 128:(a + 1) * 128] + shift
                    hi, lo = split((2.0 * one - two.T) / gap)
                    at = pl.ds(pl.multiple_of(j * n_vir + b * 128, 128), 128)
                    ahi[at, a * 128:(a + 1) * 128] = hi
                    alo[at, a * 128:(a + 1) * 128] = lo
            return 0

        lax.fori_loop(0, occ_block, amplitude, 0)

        def second(q, _):
            here = pl.ds(pl.multiple_of(q * chunk, 128), chunk)
            part = jnp.dot(jhi[here, :], ahi[...], preferred_element_type=jnp.float32)
            part += jnp.dot(jhi[here, :], alo[...], preferred_element_type=jnp.float32)
            part += jnp.dot(jlo[here, :], ahi[...], preferred_element_type=jnp.float32)
            dens[k, here, :] = part
            return 0

        lax.fori_loop(0, 4, second, 0)
        back[k, rows(me), :] = dens[k, rows(me), :]
        for h in range(PARTS):
            for n, step in enumerate(ROUTE):
                ocopy(k, n, me, dev(*step), h).start()
        return 0

    lax.fori_loop(0, occ_block, half, 0)

    for copy in hops + sent:
        copy.wait_send()
    for k in range(occ_block):
        for n, step in enumerate(ROUTE):
            xcopy(k, n, me, dev(*step)).wait_send()

    for k in range(occ_block):
        for dy, dz, dc in ((0, 0, 0),) + ROUTE:
            a = dev(4 - dy, dz, dc)
            if (dy, dz, dc) != (0, 0, 0):
                ocopy(k, 0, a, twin).wait_recv()
            for n in lanes:
                out[n, pl.ds(a * occ_block + k, depth, stride=n_occ), :] = back[k, rows(a), n * 128:(n + 1) * 128]

    for k in range(occ_block):
        for n, step in enumerate(ROUTE):
            ocopy(k, n, me, dev(*step)).wait_send()


def write(parts, held, out, sem):
    lanes, count, _ = held.shape
    step = count // parts
    copies = []
    for p in range(parts):
        for n in range(lanes):
            at = pl.ds(p * step, step)
            copies.append(pltpu.make_async_copy(held.at[n, at, :], out.at[at, n * 128:(n + 1) * 128], sem.at[p, n]))
            copies[-1].start()
    for copy in copies:
        copy.wait()


def body(integrals, occ_energy, vir_energy, orbital_order, owners):
    n_grp = lax.axis_size("grp")
    n_aux = lax.axis_size("aux")
    depth, n_occ, n_vir = integrals.shape
    occ_block = n_occ // n_aux
    total = depth * n_aux
    jb = occ_block * n_vir
    f32, bf16 = jnp.float32, jnp.bfloat16
    sizes = (n_grp, n_aux, depth, n_occ, n_vir, occ_block)
    smem = pl.BlockSpec(memory_space=pltpu.SMEM)
    vmem = pl.BlockSpec(memory_space=pltpu.VMEM)
    out = pl.pallas_call(
        lambda *refs: kernel(sizes, *refs),
        out_shape=pltpu.VMEM((n_vir // 128, depth * n_occ, 128), f32),
        in_specs=[smem, smem, smem, vmem, pl.BlockSpec(memory_space=pl.ANY)],
        out_specs=vmem,
        scratch_shapes=[
            pltpu.VMEM((n_vir // 128, depth * n_occ, 128), f32),
            pltpu.VMEM((occ_block, total, n_vir), f32),
            pltpu.VMEM((occ_block, total, n_vir), f32),
            pltpu.VMEM((total, jb), f32),
            pltpu.VMEM((depth, jb), f32),
            pltpu.VMEM((total, jb), bf16),
            pltpu.VMEM((total, jb), bf16),
            pltpu.VMEM((4, jb, 4 * depth), bf16),
            pltpu.VMEM((4, jb, 4 * depth), bf16),
            pltpu.VMEM((4 * depth, n_vir), bf16),
            pltpu.VMEM((4 * depth, n_vir), bf16),
            pltpu.VMEM((jb, n_vir), f32),
            pltpu.VMEM((jb, n_vir), bf16),
            pltpu.VMEM((jb, n_vir), bf16),
            pltpu.VMEM((n_vir, n_vir), f32),
            pltpu.VMEM((occ_block, total, n_vir), f32),
            pltpu.VMEM((occ_block, total, n_vir), f32),
            pltpu.SemaphoreType.DMA((n_vir // 128,)),
            pltpu.SemaphoreType.DMA((PIECES * 16,)),
            pltpu.SemaphoreType.DMA((PIECES, n_aux)),
            pltpu.SemaphoreType.DMA((occ_block, n_aux)),
            pltpu.SemaphoreType.DMA((occ_block, n_aux)),
            pltpu.SemaphoreType.DMA((occ_block, n_aux)),
            pltpu.SemaphoreType.DMA((occ_block, n_aux)),
        ],
        compiler_params=pltpu.CompilerParams(
            collective_id=0, has_side_effects=True, vmem_limit_bytes=50 << 20),
    )(occ_energy, orbital_order, owners, vir_energy, integrals.reshape(depth * n_occ, n_vir))
    parts = 4
    out = pl.pallas_call(
        lambda *refs: write(parts, *refs),
        out_shape=jax.ShapeDtypeStruct((depth * n_occ, n_vir), f32),
        in_specs=[vmem],
        out_specs=pl.BlockSpec(memory_space=pl.ANY),
        scratch_shapes=[pltpu.SemaphoreType.DMA((parts, n_vir // 128))],
        compiler_params=pltpu.CompilerParams(vmem_limit_bytes=8 << 20),
    )(out)
    return out.reshape(depth, n_occ, n_vir)


def solution(mesh):
    in_specs = (P("aux", "grp", None), P(), P(), P(), P())
    out_specs = P("aux", "grp", None)
    return jax.shard_map(body, mesh=mesh, in_specs=in_specs, out_specs=out_specs, check_vma=False)
```

```python
import jax
import jax.numpy as jnp
from jax import lax
from jax.experimental import pallas as pl
from jax.experimental.pallas import tpu as pltpu
from jax.sharding import PartitionSpec as P

level_shift = 0.5
MESH = pl.DeviceIdType.MESH

PIECES = 6

EVENTS = ((0, 0), (1, 0), (2, 0), (0, 1), (0, 2), (3, 0), (1, 1), (1, 2), (4, 0), (2, 1), (2, 2), (0, 3), (5, 0), (3, 1), (3, 2), (1, 3), (4, 1), (4, 2), (2, 3), (5, 1), (5, 2), (3, 3), (4, 3), (5, 3))
AHEAD = 6
AHEAD_STAGE = 10
AHEAD_SEND = 21

EARLY = (0, 6, 3)
FILL = (9, 0, 0, 0, 0, 0, 0, 0, 0, 0, 0, 0, 0, 0, 0, 0, 0, 0, 0, 0, 0, 3, 0, 0, 0)
FIRST = 3
STAGE = (0, 0, 0, 0, 0, 0, 0, 0, 0, 0, 6, 0, 0, 0, 0, 0, 0, 0, 0, 0, 0, 0, 0, 0, 0)

PARTS = 3

OUT_PARTS = 2

ROUTE = (
    (1, 0, 0), (3, 1, 0), (2, 1, 0), (0, 1, 0), (2, 0, 0),
    (1, 1, 0), (3, 0, 0), (0, 0, 1), (1, 0, 1), (3, 1, 1),
    (2, 1, 1), (0, 1, 1), (2, 0, 1), (1, 1, 1), (3, 0, 1),
)


def split(x):
    hi = x.astype(jnp.bfloat16)
    lo = (x - hi.astype(jnp.float32)).astype(jnp.bfloat16)
    return hi, lo


def kernel(sizes, occ, order, owners, vir, in_hbm, out, rows_in, staged, held, jblock, jcut, jhi, jlo,
           jthi, jtlo, xhi, xlo, acc, ahi, alo, vsum, dens, back, load_sem, jsend, jrecv, xsend, xrecv,
           osend, orecv):
    n_grp, n_aux, depth, n_occ, n_vir, occ_block = sizes
    chunk = 4 * depth
    grp = lax.axis_index("grp")
    me = lax.axis_index("aux")
    y, z, c = lax.div(me, 4), lax.rem(lax.div(me, 2), 2), lax.rem(me, 2)
    nxt = lax.rem(grp + 1, n_grp)
    prv = lax.rem(grp + n_grp - 1, n_grp)

    def dev(dy, dz, dc):
        return lax.rem(y + dy, 4) * 4 + lax.rem(z + dz, 2) * 2 + lax.rem(c + dc, 2)

    def swap(group):
        return 1 - jnp.minimum(lax.rem(group, 4), 1)

    def shard(dy, dz, dc):
        return dev(dy, dz + swap(grp), dc)

    def rows(a):
        return pl.ds(pl.multiple_of(a * depth, 8), depth)

    lanes = range(n_vir // 128)
    loads = [pltpu.make_async_copy(in_hbm.at[:, n * 128:(n + 1) * 128], rows_in.at[n], load_sem.at[n]) for n in lanes]
    for load in loads:
        load.start()
    barrier = pltpu.get_barrier_semaphore()
    for n in range(1, 16):
        pl.semaphore_signal(barrier, inc=1, device_id=(grp, lax.rem(me + n, 16)), device_id_type=MESH)
    pl.semaphore_signal(barrier, inc=1, device_id=(nxt, dev(0, swap(nxt), 0)), device_id_type=MESH)
    pl.semaphore_signal(barrier, inc=1, device_id=(prv, shard(0, 0, 0)), device_id_type=MESH)

    wide = jnp.broadcast_to(vir[...][None, :], (n_vir, n_vir))
    vsum[...] = wide + wide.T
    for load in loads:
        load.wait()

    picked = owners[0, nxt] * occ_block
    for k in range(occ_block):
        for n in lanes:
            at = k * n_vir + n * 128
            jcut[:, at:at + 128] = rows_in[n, pl.ds(picked + k, depth, stride=n_occ), :]

    piece = depth // PIECES

    def jcopy(n, p, a, target, src=None):
        at = pl.ds(pl.multiple_of(a * depth + p * piece, 8), piece)
        return pltpu.make_async_remote_copy(
            src_ref=jblock.at[at, :] if src is None else src, dst_ref=jblock.at[at, :],
            send_sem=jsend.at[n], recv_sem=jrecv.at[p, a], device_id=target, device_id_type=MESH)

    def part(a, h, parts=PARTS):
        size = depth // parts
        return rows(a) if h is None else pl.ds(pl.multiple_of(a * depth + h * size, 8), size)

    def xcopy(k, n, a, target, h=None):
        return pltpu.make_async_remote_copy(
            src_ref=staged.at[k, part(target, h), :], dst_ref=held.at[k, part(a, h), :],
            send_sem=xsend.at[k, n], recv_sem=xrecv.at[k, a], device_id=(grp, target), device_id_type=MESH)

    def ocopy(k, n, a, target, h=None):
        return pltpu.make_async_remote_copy(
            src_ref=dens.at[k, part(target, h, OUT_PARTS), :], dst_ref=back.at[k, part(a, h, OUT_PARTS), :],
            send_sem=osend.at[k, n], recv_sem=orecv.at[k, a], device_id=(grp, target), device_id_type=MESH)

    def stage(k, a):
        for n in lanes:
            staged[k, rows(a), n * 128:(n + 1) * 128] = rows_in[n, pl.ds(a * occ_block + k, depth, stride=n_occ), :]

    first = [(0, n, h) for h in range(PARTS) for n in EARLY]
    xorder = first + [e for e in [(k, n, h) for k in range(occ_block) for h in range(PARTS) for n in range(15)]
                      if e not in first]
    blocks = [(0, n) for n in EARLY] + [(0, n) for n in range(15) if n not in EARLY] + [(1, n) for n in range(15)]
    done = [0]
    ready = [0]

    def stage_all(chosen):
        for k, n in chosen:
            stage(k, dev(*ROUTE[n]))

    def send_all(chosen):
        for k, n, h in chosen:
            xcopy(k, n, me, dev(*ROUTE[n]), h).start()

    def xstage(count):
        stage_all(blocks[ready[0]:ready[0] + count])
        ready[0] += count

    def xsend_some(count):
        send_all(xorder[done[0]:done[0] + count])
        done[0] += count

    xstage(FIRST)
    pl.semaphore_wait(barrier, 17)
    hops = [jcopy(p, p, me, (nxt, dev(0, swap(nxt), 0)), jcut.at[p * piece:(p + 1) * piece, :]) for p in range(PIECES)]
    for hop in hops:
        hop.start()

    up, down, over, twin = dev(1, 0, 0), dev(3, 0, 0), dev(0, 1, 0), dev(0, 0, 1)
    own = (shard(0, 0, 0), (up, down, over))
    opposite, above, below, across = shard(0, 1, 0), shard(1, 0, 0), shard(3, 0, 0), shard(1, 1, 0)
    rest = ((shard(3, 1, 0), ()), (shard(2, 0, 0), ()), (shard(2, 1, 0), ()))
    by_y = (own, (opposite, (up, down)), (below, (up,)), (across, (down,)), (above, ())) + rest
    by_z = (own, (below, (over, up)), (above, (over,)), (across, (down,)), (opposite, ())) + rest
    plans = (by_z, by_y, by_z) * 2
    sent = []

    def jrelay(p, event):
        a, targets = plans[p][event]
        jcopy(0, p, a, (grp, twin)).wait_recv()
        for t in targets + (twin,):
            copy = jcopy(len(sent) + PIECES, p, a, (grp, t))
            copy.start()
            sent.append(copy)

    xsend_some(FILL[0])
    xstage(STAGE[0])
    later = (blocks[ready[0]:ready[0] + AHEAD], xorder[done[0]:done[0] + AHEAD])
    ready[0] += AHEAD
    done[0] += AHEAD

    @pl.when(grp == 0)
    def _():
        stage_all(later[0])
        send_all(later[1])

    for at, (p, event) in enumerate(EVENTS):
        jrelay(p, event)
        if at + 1 == AHEAD_STAGE:
            pl.when(grp != 0)(lambda: stage_all(later[0]))
        if at + 1 == AHEAD_SEND:
            pl.when(grp != 0)(lambda: send_all(later[1]))
        xsend_some(FILL[at + 1])
        xstage(STAGE[at + 1])
    xsend_some(15 * PARTS - done[0])
    xstage(30 - ready[0])
    xsend_some(30 * PARTS - done[0])
    for k in range(occ_block):
        for n in lanes:
            held[k, rows(me), n * 128:(n + 1) * 128] = rows_in[
                n, pl.ds(me * occ_block + k, depth, stride=n_occ), :]
    for event in range(4, 8):
        for p in range(PIECES):
            jrelay(p, event)

    def prepare(q, _):
        for zz in range(2):
            a = q * 4 + zz * 2 + lax.rem(c + 1, 2)
            for p in range(PIECES):
                jcopy(0, p, a, (grp, twin)).wait_recv()
        base = pl.multiple_of(q * chunk, 128)
        here = pl.ds(base, chunk)
        for m in range(chunk // 128):
            part = pl.ds(pl.multiple_of(base + m * 128, 128), 128)
            hi, lo = split(jblock[part, :])
            jhi[part, :] = hi
            jlo[part, :] = lo
        for n in range(occ_block * n_vir // 128):
            hi, lo = split(jblock[here, n * 128:(n + 1) * 128].T)
            jthi[q, n * 128:(n + 1) * 128, :] = hi
            jtlo[q, n * 128:(n + 1) * 128, :] = lo
        return 0

    lax.fori_loop(0, 4, prepare, 0)

    def half(k, _):
        acc[...] = jnp.zeros_like(acc)

        def first(q, _):
            for m in range(4):
                a = q * 4 + m

                @pl.when(a != me)
                def _():
                    xcopy(k, 0, a, twin).wait_recv()
            for m in range(4):
                hi, lo = split(held[k, rows(q * 4 + m), :])
                xhi[m * depth:(m + 1) * depth, :] = hi
                xlo[m * depth:(m + 1) * depth, :] = lo
            acc[...] += jnp.dot(jthi[q], xhi[...], preferred_element_type=jnp.float32)
            acc[...] += jnp.dot(jthi[q], xlo[...], preferred_element_type=jnp.float32)
            acc[...] += jnp.dot(jtlo[q], xhi[...], preferred_element_type=jnp.float32)
            return 0

        lax.fori_loop(0, 4, first, 0)
        level_i = occ[order[grp * n_occ + me * occ_block + k]]

        def amplitude(j, _):
            level_j = occ[order[prv * n_occ + owners[0, grp] * occ_block + j]]
            shift = level_shift - level_i - level_j
            for b in range(n_vir // 128):
                for a in range(n_vir // 128):
                    one = acc[pl.ds(pl.multiple_of(j * n_vir + b * 128, 128), 128), a * 128:(a + 1) * 128]
                    two = acc[pl.ds(pl.multiple_of(j * n_vir + a * 128, 128), 128), b * 128:(b + 1) * 128]
                    gap = vsum[b * 128:(b + 1) * 128, a * 128:(a + 1) * 128] + shift
                    hi, lo = split((2.0 * one - two.T) / gap)
                    at = pl.ds(pl.multiple_of(j * n_vir + b * 128, 128), 128)
                    ahi[at, a * 128:(a + 1) * 128] = hi
                    alo[at, a * 128:(a + 1) * 128] = lo
            return 0

        lax.fori_loop(0, occ_block, amplitude, 0)

        def second(q, _):
            here = pl.ds(pl.multiple_of(q * chunk, 128), chunk)
            part = jnp.dot(jhi[here, :], ahi[...], preferred_element_type=jnp.float32)
            part += jnp.dot(jhi[here, :], alo[...], preferred_element_type=jnp.float32)
            part += jnp.dot(jlo[here, :], ahi[...], preferred_element_type=jnp.float32)
            dens[k, here, :] = part
            return 0

        lax.fori_loop(0, 4, second, 0)
        back[k, rows(me), :] = dens[k, rows(me), :]
        for h in range(OUT_PARTS):
            for n, step in enumerate(ROUTE):
                ocopy(k, n, me, dev(*step), h).start()
        return 0

    lax.fori_loop(0, occ_block, half, 0)

    for copy in hops + sent:
        copy.wait_send()
    for k in range(occ_block):
        for n, step in enumerate(ROUTE):
            xcopy(k, n, me, dev(*step)).wait_send()

    for k in range(occ_block):
        for dy, dz, dc in ((0, 0, 0),) + ROUTE:
            a = dev(4 - dy, dz, dc)
            if (dy, dz, dc) != (0, 0, 0):
                ocopy(k, 0, a, twin).wait_recv()
            for n in lanes:
                out[n, pl.ds(a * occ_block + k, depth, stride=n_occ), :] = back[k, rows(a), n * 128:(n + 1) * 128]

    for k in range(occ_block):
        for n, step in enumerate(ROUTE):
            ocopy(k, n, me, dev(*step)).wait_send()


def write(parts, held, out, sem):
    lanes, count, _ = held.shape
    step = count // parts
    copies = []
    for p in range(parts):
        for n in range(lanes):
            at = pl.ds(p * step, step)
            copies.append(pltpu.make_async_copy(held.at[n, at, :], out.at[at, n * 128:(n + 1) * 128], sem.at[p, n]))
            copies[-1].start()
    for copy in copies:
        copy.wait()


def body(integrals, occ_energy, vir_energy, orbital_order, owners):
    n_grp = lax.axis_size("grp")
    n_aux = lax.axis_size("aux")
    depth, n_occ, n_vir = integrals.shape
    occ_block = n_occ // n_aux
    total = depth * n_aux
    jb = occ_block * n_vir
    f32, bf16 = jnp.float32, jnp.bfloat16
    sizes = (n_grp, n_aux, depth, n_occ, n_vir, occ_block)
    smem = pl.BlockSpec(memory_space=pltpu.SMEM)
    vmem = pl.BlockSpec(memory_space=pltpu.VMEM)
    out = pl.pallas_call(
        lambda *refs: kernel(sizes, *refs),
        out_shape=pltpu.VMEM((n_vir // 128, depth * n_occ, 128), f32),
        in_specs=[smem, smem, smem, vmem, pl.BlockSpec(memory_space=pl.ANY)],
        out_specs=vmem,
        scratch_shapes=[
            pltpu.VMEM((n_vir // 128, depth * n_occ, 128), f32),
            pltpu.VMEM((occ_block, total, n_vir), f32),
            pltpu.VMEM((occ_block, total, n_vir), f32),
            pltpu.VMEM((total, jb), f32),
            pltpu.VMEM((depth, jb), f32),
            pltpu.VMEM((total, jb), bf16),
            pltpu.VMEM((total, jb), bf16),
            pltpu.VMEM((4, jb, 4 * depth), bf16),
            pltpu.VMEM((4, jb, 4 * depth), bf16),
            pltpu.VMEM((4 * depth, n_vir), bf16),
            pltpu.VMEM((4 * depth, n_vir), bf16),
            pltpu.VMEM((jb, n_vir), f32),
            pltpu.VMEM((jb, n_vir), bf16),
            pltpu.VMEM((jb, n_vir), bf16),
            pltpu.VMEM((n_vir, n_vir), f32),
            pltpu.VMEM((occ_block, total, n_vir), f32),
            pltpu.VMEM((occ_block, total, n_vir), f32),
            pltpu.SemaphoreType.DMA((n_vir // 128,)),
            pltpu.SemaphoreType.DMA((PIECES * 16,)),
            pltpu.SemaphoreType.DMA((PIECES, n_aux)),
            pltpu.SemaphoreType.DMA((occ_block, n_aux)),
            pltpu.SemaphoreType.DMA((occ_block, n_aux)),
            pltpu.SemaphoreType.DMA((occ_block, n_aux)),
            pltpu.SemaphoreType.DMA((occ_block, n_aux)),
        ],
        compiler_params=pltpu.CompilerParams(
            collective_id=0, has_side_effects=True, vmem_limit_bytes=50 << 20),
    )(occ_energy, orbital_order, owners, vir_energy, integrals.reshape(depth * n_occ, n_vir))
    parts = 4
    out = pl.pallas_call(
        lambda *refs: write(parts, *refs),
        out_shape=jax.ShapeDtypeStruct((depth * n_occ, n_vir), f32),
        in_specs=[vmem],
        out_specs=pl.BlockSpec(memory_space=pl.ANY),
        scratch_shapes=[pltpu.SemaphoreType.DMA((parts, n_vir // 128))],
        compiler_params=pltpu.CompilerParams(vmem_limit_bytes=8 << 20),
    )(out)
    return out.reshape(depth, n_occ, n_vir)


def solution(mesh):
    in_specs = (P("aux", "grp", None), P(), P(), P(), P())
    out_specs = P("aux", "grp", None)
    return jax.shard_map(body, mesh=mesh, in_specs=in_specs, out_specs=out_specs, check_vma=False)
```
